32 devices in a mesh: dp: 8 (over y, x, core), tensor: 4 (over z).
Axes of the slice: x: 2, y: 2, z: 4, core: 2. Of those that a mesh axis runs over, the one named last changes fastest.
Arguments:
- tokens: bfloat16 [16384, 2048], P(('dp', 'tensor'))
- teacher: bfloat16 [16384, 2048], P(('dp', 'tensor')), may hold values from -6 to 6
- valid: int32 [16384], P(('dp', 'tensor')), may hold values from 0 to 1, as said below
- prefix: int32 [16], P('dp'), may hold values from 102 to 512, as said below
- w_query: bfloat16 [2048, 1024], P(None, 'tensor'), may hold values from -0.125 to 0.125
- key_weight: bfloat16 [2048, 256], replicated, may hold values from -0.125 to 0.125
- value_weight: bfloat16 [2048, 256], replicated, may hold values from -0.125 to 0.125
- query_gain: float32 [64], replicated, may hold values from 0.25 to 1.75
- key_gain: float32 [64], replicated, may hold values from 0.25 to 1.75
- w_out: bfloat16 [1024, 2048], P('tensor'), may hold values from -3 to 3
- attn_gain: float32 [2048], replicated, may hold values from 0.25 to 1.75
- ffn_gain: float32 [2048], replicated, may hold values from 0.25 to 1.75
- w_gate: bfloat16 [2048, 5120], P(None, 'tensor'), may hold values from -0.125 to 0.125
- w_up: bfloat16 [2048, 5120], P(None, 'tensor'), may hold values from -0.125 to 0.125
- w_down: bfloat16 [5120, 2048], P('tensor'), may hold values from -0.078125 to 0.078125
Outputs:
- output: bfloat16 [16384, 2048], P(('dp', 'tensor'))
- loss: float32 [], replicated
- grad_tokens: float32 [16384, 2048], P(('dp', 'tensor'))
- grad_query: float32 [2048, 1024], P(None, 'tensor')
- grad_key: float32 [2048, 256], replicated
- grad_value: float32 [2048, 256], replicated
- grad_query_gain: float32 [64], replicated
- grad_key_gain: float32 [64], replicated
- grad_out: float32 [1024, 2048], P('tensor')
- grad_attn_gain: float32 [2048], replicated
- grad_ffn_gain: float32 [2048], replicated
- grad_gate: float32 [2048, 5120], P(None, 'tensor')
- grad_up: float32 [2048, 5120], P(None, 'tensor')
- grad_down: float32 [5120, 2048], P('tensor')
The draws below stay inside these ranges and needn't reach their ends.
Inputs may be any that keep to these rules, and one draw needn't show every extreme that they name: The first token of every sequence is valid. One sequence has prefix length exactly 512 and another exactly 102.
All inputs are finite; a program needn't handle non-finite values.
Results may differ from the reference program's by a relative error of at most 0.015.
Values may be sent and summed in bfloat16 or wider, within the bound.
A program may use at most 256 MiB of HBM per device.

```python
import math
import jax
import jax.numpy as jnp
from jax import lax

MODEL_WIDTH = 2048
QUERY_HEADS = 16
KEY_VALUE_HEADS = 4
HEAD_SIZE = 64
FF = 5120
SEQ_LEN = 1024
SEQS = 16
TOKENS = 16384


def draw_tokens(key, part):
    key_base, key_matrix, key_cols = jax.random.split(key, 3)
    values_raw = jax.random.normal(key_base, (TOKENS, MODEL_WIDTH), jnp.float32)
    row_scale = jnp.exp(jax.random.uniform(key_matrix, (TOKENS, 1), jnp.float32, math.log(0.3), math.log(3.0)))
    col_scale = jnp.exp(jax.random.uniform(key_cols, (1, MODEL_WIDTH), jnp.float32, math.log(0.4), math.log(4.0)))
    return (values_raw * row_scale * col_scale).astype(jnp.bfloat16)


def draw_valid(key, part):
    seq_ids = jnp.arange(TOKENS) // SEQ_LEN
    positions = jnp.arange(TOKENS) % SEQ_LEN
    threshold = 250 + 500 * seq_ids // max(SEQS - 1, 1)
    draws_int = jax.random.randint(key, (TOKENS,), 0, 1000)
    return jnp.where((draws_int < threshold) | (positions == 0), 1, 0).astype(jnp.int32)


def draw_prefix(key, part):
    key_len, key_perm = jax.random.split(key, 2)
    lengths = jax.random.randint(key_len, (SEQS,), SEQ_LEN // 10, SEQ_LEN // 2 + 1)
    shuffle = jax.random.permutation(key_perm, SEQS)
    lengths = jnp.where(shuffle == 0, SEQ_LEN // 2, lengths)
    lengths = jnp.where(shuffle == 1, SEQ_LEN // 10, lengths)
    return lengths.astype(jnp.int32)


def steps_of(own_key, extent, cuts, least, largest):
    loudness = 1.0
    for axis_at, parts in cuts:
        steps = jax.random.uniform(jax.random.fold_in(jax.random.fold_in(own_key, 6), axis_at), (parts,), jnp.float32, least / len(cuts), largest / len(cuts))
        loudness = loudness * jnp.repeat(jnp.exp(steps), extent[axis_at] // parts).reshape((-1,) + (1,) * (len(extent) - 1 - axis_at))
    return loudness


def scatter_about(stream_key, dims, spread, limit, cuts=(), kind=jnp.bfloat16):
    values = jax.random.normal(stream_key, dims, jnp.float32) * spread
    if len(cuts) > 0:
        values = steps_of(stream_key, dims, cuts, -0.22, 0.18) * values
    return jnp.clip(values, min=-limit, max=limit).astype(kind)


def setup_inputs(seed: int = 0) -> dict:
    key_list = jax.random.split(jax.random.key(seed), 16)
    tokens = draw_tokens(jax.random.fold_in(key_list[15], 71), 0)
    teacher = scatter_about(key_list[1], (TOKENS, MODEL_WIDTH), 1.0, 6.0, ((0, 32),))
    valid = draw_valid(jax.random.fold_in(key_list[15], 71), 0)
    prefix = draw_prefix(jax.random.fold_in(key_list[15], 71), 0)
    w_query = scatter_about(key_list[4], (MODEL_WIDTH, QUERY_HEADS * HEAD_SIZE), MODEL_WIDTH ** -0.5, 0.125, ((1, 4),))
    key_weight = scatter_about(key_list[5], (MODEL_WIDTH, KEY_VALUE_HEADS * HEAD_SIZE), MODEL_WIDTH ** -0.5, 0.125)
    value_weight = scatter_about(key_list[6], (MODEL_WIDTH, KEY_VALUE_HEADS * HEAD_SIZE), MODEL_WIDTH ** -0.5, 0.125)
    query_gain = jnp.clip(1.0 + 0.15 * jax.random.normal(key_list[7], (HEAD_SIZE,), jnp.float32), 0.25, 1.75)
    key_gain = jnp.clip(1.0 + 0.15 * jax.random.normal(key_list[8], (HEAD_SIZE,), jnp.float32), 0.25, 1.75)
    w_out = scatter_about(key_list[9], (QUERY_HEADS * HEAD_SIZE, MODEL_WIDTH), 4 ** -0.5, 3.0, ((0, 4),))
    attn_gain = jnp.clip(1.0 + 0.15 * jax.random.normal(key_list[10], (MODEL_WIDTH,), jnp.float32), 0.25, 1.75)
    ffn_gain = jnp.clip(1.0 + 0.15 * jax.random.normal(key_list[11], (MODEL_WIDTH,), jnp.float32), 0.25, 1.75)
    w_gate = scatter_about(key_list[12], (MODEL_WIDTH, FF), MODEL_WIDTH ** -0.5, 0.125, ((1, 4),))
    w_up = scatter_about(key_list[13], (MODEL_WIDTH, FF), MODEL_WIDTH ** -0.5, 0.125, ((1, 4),))
    w_down = scatter_about(key_list[14], (FF, MODEL_WIDTH), FF ** -0.5, 0.078125, ((0, 4),))
    return dict(tokens=tokens, teacher=teacher, valid=valid, prefix=prefix, w_query=w_query, key_weight=key_weight, value_weight=value_weight, query_gain=query_gain, key_gain=key_gain, w_out=w_out, attn_gain=attn_gain, ffn_gain=ffn_gain, w_gate=w_gate, w_up=w_up, w_down=w_down)


@jax.custom_vjp
def lowered_cast(v):
    return lax.optimization_barrier(v.astype(jnp.bfloat16)).astype(jnp.float32)

@jax.custom_vjp
def lowered_cast_backward(v):
    return v

def low_keep(v):
    return (lowered_cast(v), None)

def low_pass(kept, grad):
    return (grad,)

def back_keep(v):
    return (v, None)

def back_low(kept, grad):
    return (lowered_cast(grad),)
lowered_cast.defvjp(low_keep, low_pass)
lowered_cast_backward.defvjp(back_keep, back_low)
EPSILON = 1e-06
EXACT_PRECISION = lax.Precision.HIGHEST

def rope_tables(sequence_length, head_size):
    half_size = head_size // 2
    frequency = 10000.0 ** (-2.0 * jnp.arange(half_size, dtype=jnp.float32) / head_size)
    angles = jnp.arange(sequence_length, dtype=jnp.float32)[:, None] * frequency[None, :]
    cosine = jnp.concatenate([jnp.cos(angles), jnp.cos(angles)], 1)
    sine_tab = jnp.concatenate([jnp.sin(angles), jnp.sin(angles)], 1)
    return (cosine, sine_tab)

def rotate(vector, cosine, sine_tab):
    half_size = vector.shape[-1] // 2
    turned = jnp.concatenate([-vector[..., half_size:], vector[..., :half_size]], -1)
    return vector * cosine + turned * sine_tab

def rms_norm(vector, gain_vec):
    return vector * lax.rsqrt(lax.optimization_barrier(jnp.mean(vector * vector, axis=-1, keepdims=True)) + EPSILON) * gain_vec

def block_forward(seq_rows, params, prefix_len):
    w_query, key_weight, value_weight, query_gain, key_gain, w_out, attn_gain, ffn_gain, w_gate, w_up, w_down = params
    sequence_length = seq_rows.shape[0]
    normed_input = lowered_cast(rms_norm(seq_rows, attn_gain))
    query_matrix = lowered_cast_backward(jnp.dot(normed_input, w_query, precision=EXACT_PRECISION)).reshape(sequence_length, QUERY_HEADS, HEAD_SIZE)
    key_matrix = lowered_cast_backward(jnp.dot(normed_input, key_weight, precision=EXACT_PRECISION)).reshape(sequence_length, KEY_VALUE_HEADS, HEAD_SIZE)
    value_matrix = lowered_cast(lowered_cast_backward(jnp.dot(normed_input, value_weight, precision=EXACT_PRECISION))).reshape(sequence_length, KEY_VALUE_HEADS, HEAD_SIZE)
    cosine, sine_tab = rope_tables(sequence_length, HEAD_SIZE)
    query_matrix = lowered_cast(rotate(rms_norm(query_matrix, query_gain), cosine[:, None, :], sine_tab[:, None, :]))
    key_matrix = lowered_cast(rotate(rms_norm(key_matrix, key_gain), cosine[:, None, :], sine_tab[:, None, :]))
    grouped_heads = query_matrix.reshape(sequence_length, KEY_VALUE_HEADS, QUERY_HEADS // KEY_VALUE_HEADS, HEAD_SIZE)
    scores = lowered_cast_backward(jnp.einsum('ikgd,jkd->kgij', grouped_heads, key_matrix, precision=EXACT_PRECISION) * HEAD_SIZE ** (-0.5))
    row_pos = jnp.arange(sequence_length)[:, None]
    col_pos = jnp.arange(sequence_length)[None, :]
    allowed = (col_pos <= row_pos) | (row_pos < prefix_len) & (col_pos < prefix_len)
    scores = jnp.where(allowed, scores, -1e+30)
    row_max = lax.optimization_barrier(jnp.max(scores, -1, keepdims=True))
    weights = jnp.where(allowed, jnp.exp(scores - row_max), 0.0)
    attn_probs = weights / lax.optimization_barrier(jnp.sum(weights, -1, keepdims=True))
    attended = jnp.einsum('kgij,jkd->ikgd', lowered_cast(attn_probs), value_matrix, precision=EXACT_PRECISION)
    attended = lowered_cast(lowered_cast_backward(attended.reshape(sequence_length, QUERY_HEADS * HEAD_SIZE)))
    middle = seq_rows + lowered_cast_backward(jnp.dot(attended, w_out, precision=EXACT_PRECISION))
    normed_two = lowered_cast(rms_norm(middle, ffn_gain))
    gate_act = lowered_cast_backward(jnp.dot(normed_two, w_gate, precision=EXACT_PRECISION))
    up_act = lowered_cast_backward(jnp.dot(normed_two, w_up, precision=EXACT_PRECISION))
    hidden = lowered_cast(gate_act * jax.nn.sigmoid(gate_act) * up_act)
    return middle + lowered_cast_backward(jnp.dot(hidden, w_down, precision=EXACT_PRECISION))

def reference(tokens, teacher, valid, prefix, w_query, key_weight, value_weight, query_gain, key_gain, w_out, attn_gain, ffn_gain, w_gate, w_up, w_down):
    params = tuple((p.astype(jnp.float32) for p in (w_query, key_weight, value_weight, query_gain, key_gain, w_out, attn_gain, ffn_gain, w_gate, w_up, w_down)))
    valid_count = jnp.sum(valid).astype(jnp.float32)
    loss_scale = SEQS * SEQ_LEN / valid_count
    seq_inputs = tokens.astype(jnp.float32).reshape(SEQS, SEQ_LEN, MODEL_WIDTH)
    seq_targets = teacher.astype(jnp.float32).reshape(SEQS, SEQ_LEN, MODEL_WIDTH)
    seq_masks = valid.astype(jnp.float32).reshape(SEQS, SEQ_LEN)

    def one_sequence(running, packed):
        totals, squares = running
        seq_rows, seq_target, seq_mask, prefix_len = packed
        result, pullback = jax.vjp(lambda seq_input, weights_in: block_forward(seq_input, weights_in, prefix_len), seq_rows, params)
        error_rows = result - seq_target
        cotangent = loss_scale * error_rows * seq_mask[:, None]
        grad_rows, grad_params = pullback(cotangent)
        totals = jax.tree.map(lambda left, right: left + right, totals, grad_params)
        squares = squares + jnp.sum(error_rows * error_rows * seq_mask[:, None])
        return ((totals, squares), (result, grad_rows))
    zero_grads = jax.tree.map(jnp.zeros_like, params)
    (grads, squares), (results, grad_rows) = lax.scan(one_sequence, (zero_grads, jnp.zeros((), jnp.float32)), (seq_inputs, seq_targets, seq_masks, prefix))
    loss = squares / (valid_count * MODEL_WIDTH)
    return (results.reshape(SEQS * SEQ_LEN, MODEL_WIDTH).astype(jnp.bfloat16), loss, grad_rows.reshape(SEQS * SEQ_LEN, MODEL_WIDTH), grads[0], grads[1], grads[2], grads[3], grads[4], grads[5], grads[6], grads[7], grads[8], grads[9], grads[10])
```

```python
import jax
import jax.numpy as jnp
from jax import lax
from jax.sharding import PartitionSpec as P

QUERY_HEADS = 16
KEY_VALUE_HEADS = 4
HEAD_SIZE = 64
SEQ_LEN = 1024
GROUP = QUERY_HEADS // KEY_VALUE_HEADS
EPSILON = 1e-06
BF = jnp.bfloat16
F32 = jnp.float32


def rope_rows(start, rows):
    half = HEAD_SIZE // 2
    frequency = 10000.0 ** (-2.0 * jnp.arange(half, dtype=F32) / HEAD_SIZE)
    angles = (start + jnp.arange(rows)).astype(F32)[:, None] * frequency[None, :]
    cosine = jnp.concatenate([jnp.cos(angles), jnp.cos(angles)], 1)
    sine = jnp.concatenate([jnp.sin(angles), jnp.sin(angles)], 1)
    return cosine[:, None, :], sine[:, None, :]


def rotate(vector, cosine, sine):
    half = vector.shape[-1] // 2
    turned = jnp.concatenate([-vector[..., half:], vector[..., :half]], -1)
    return vector * cosine + turned * sine


def unrotate(gradient, cosine, sine):
    half = gradient.shape[-1] // 2
    shifted = gradient * sine
    return gradient * cosine + jnp.concatenate([shifted[..., half:], -shifted[..., :half]], -1)


def inv_root(vector):
    return lax.rsqrt(jnp.mean(vector * vector, axis=-1, keepdims=True) + EPSILON)


def norm_back(gradient, source, factor, gain):
    scaled = gradient * gain
    return factor * scaled - source * factor**3 * jnp.mean(scaled * source, axis=-1, keepdims=True)


def dot(a, b):
    return jnp.dot(a, b, preferred_element_type=F32)


def dot_t(a, b):
    return lax.dot_general(a, b, (((1,), (1,)), ((), ())), preferred_element_type=F32)


def t_dot(a, b):
    return lax.dot_general(a, b, (((0,), (0,)), ((), ())), preferred_element_type=F32)


def seen(start, rows, prefix_len):
    row = start + jnp.arange(rows)[:, None]
    col = jnp.arange(SEQ_LEN)[None, :]
    return (col <= row) | (row < prefix_len) & (col < prefix_len)


def attend(q, k, v, start, prefix_len):
    rows = q.shape[0]
    grouped = q.reshape(rows, KEY_VALUE_HEADS, GROUP, HEAD_SIZE)
    scores = jnp.einsum("ikgd,jkd->kgij", grouped, k, preferred_element_type=F32) * HEAD_SIZE**-0.5
    allowed = seen(start, rows, prefix_len)
    scores = jnp.where(allowed, scores, -1e30)
    top = jnp.max(scores, -1, keepdims=True)
    weights = jnp.where(allowed, jnp.exp(scores - top), 0.0)
    total = jnp.sum(weights, -1, keepdims=True)
    probs = (weights / total).astype(BF)
    attended = jnp.einsum("kgij,jkd->ikgd", probs, v, preferred_element_type=F32)
    return attended.reshape(rows, QUERY_HEADS * HEAD_SIZE), (top + jnp.log(total))[..., 0]


def attend_back(q, k, v, start, prefix_len, lse, grad):
    rows = q.shape[0]
    scale = HEAD_SIZE**-0.5
    grouped = q.reshape(rows, KEY_VALUE_HEADS, GROUP, HEAD_SIZE)
    scores = jnp.einsum("ikgd,jkd->kgij", grouped, k, preferred_element_type=F32) * scale
    allowed = seen(start, rows, prefix_len)
    probs = jnp.where(allowed, jnp.exp(jnp.where(allowed, scores, -1e30) - lse[..., None]), 0.0)
    heads = grad.reshape(rows, KEY_VALUE_HEADS, GROUP, HEAD_SIZE)
    dprobs = jnp.einsum("ikgd,jkd->kgij", heads, v, preferred_element_type=F32)
    inner = jnp.sum(probs * dprobs, -1, keepdims=True)
    dscores = (probs * (dprobs - inner)).astype(BF)
    dq = jnp.einsum("kgij,jkd->ikgd", dscores, k, preferred_element_type=F32) * scale
    dk = jnp.einsum("kgij,ikgd->jkd", dscores, grouped, preferred_element_type=F32) * scale
    dv = jnp.einsum("kgij,ikgd->jkd", probs.astype(BF), heads, preferred_element_type=F32)
    return dq.reshape(rows, QUERY_HEADS, HEAD_SIZE), dk, dv


def sum_small(vector):
    return jnp.sum(lax.all_gather(vector[None], ("dp", "tensor"), axis=0, tiled=True), 0)


def body(
    tokens,
    teacher,
    valid,
    prefix,
    w_query,
    key_weight,
    value_weight,
    query_gain,
    key_gain,
    w_out,
    attn_gain,
    ffn_gain,
    w_gate,
    w_up,
    w_down,
):
    rows, width = tokens.shape
    dp_size, t_size = lax.axis_size("dp"), lax.axis_size("tensor")
    dp_at, t_at = lax.axis_index("dp"), lax.axis_index("tensor")
    per_seq = SEQ_LEN // rows
    seq_groups = [list(range(g, g + per_seq)) for g in range(0, t_size, per_seq)]
    start = t_at % per_seq * rows
    prefix_len = prefix[t_at // per_seq]
    q_all = QUERY_HEADS * HEAD_SIZE
    kv_all = KEY_VALUE_HEADS * HEAD_SIZE
    q_dev = w_query.shape[1]
    cut = width // dp_size

    count = sum_small(jnp.broadcast_to(jnp.sum(valid).astype(F32), (128,)))[0]

    query_cut = lax.dynamic_slice_in_dim(w_query, dp_at * cut, cut, 0)
    query_full = (
        lax.all_gather(query_cut, ("dp", "tensor"), axis=0, tiled=False)
        .reshape(dp_size, t_size, cut, q_dev)
        .transpose(0, 2, 1, 3)
        .reshape(width, q_all)
    )
    out_rows = w_out.shape[0] // dp_size
    out_cut = lax.dynamic_slice_in_dim(w_out, dp_at * out_rows, out_rows, 0)
    out_full = lax.all_gather(out_cut, ("tensor", "dp"), axis=0, tiled=True)

    source = tokens.astype(F32)
    factor_one = inv_root(source)
    normed = (source * factor_one * attn_gain).astype(BF)
    k_raw = dot(normed, key_weight).reshape(rows, KEY_VALUE_HEADS, HEAD_SIZE)
    v_low = dot(normed, value_weight).astype(BF)
    cosine, sine = rope_rows(start, rows)
    k_factor = inv_root(k_raw)
    k_low = rotate(k_raw * k_factor * key_gain, cosine, sine).astype(BF).reshape(rows, kv_all)
    kv_seq = lax.all_gather(
        jnp.concatenate([k_low, v_low], 1),
        "tensor",
        axis=0,
        tiled=True,
        axis_index_groups=seq_groups,
    )
    k_seq = kv_seq[:, :kv_all].reshape(SEQ_LEN, KEY_VALUE_HEADS, HEAD_SIZE)
    v_seq = kv_seq[:, kv_all:].reshape(SEQ_LEN, KEY_VALUE_HEADS, HEAD_SIZE)
    q_raw = dot(normed, query_full).reshape(rows, QUERY_HEADS, HEAD_SIZE)
    q_factor = inv_root(q_raw)
    q_low = rotate(q_raw * q_factor * query_gain, cosine, sine).astype(BF)
    attended, lse = attend(q_low, k_seq, v_seq, start, prefix_len)
    attended = attended.astype(BF)
    middle = source + dot(attended, out_full)

    factor_two = inv_root(middle)
    normed_two = (middle * factor_two * ffn_gain).astype(BF)
    normed_two_all = lax.all_gather(normed_two, "tensor", axis=0, tiled=True)
    gate = dot(normed_two_all, w_gate)
    up = dot(normed_two_all, w_up)
    sig = jax.nn.sigmoid(gate)
    hidden = (gate * sig * up).astype(BF)
    result = middle + lax.psum_scatter(
        dot(hidden, w_down).astype(BF), "tensor", scatter_dimension=0, tiled=True
    ).astype(F32)
    mask = valid.astype(F32)[:, None]
    error = result - teacher.astype(F32)
    squares = jnp.sum(error * error * mask)
    cot = (rows * t_size * dp_size / count) * error * mask
    cot_all = lax.all_gather(cot.astype(BF), "tensor", axis=0, tiled=True)
    grad_down = t_dot(hidden, cot_all)
    dhidden = dot_t(cot_all, w_down)
    dgate = (dhidden * up * sig * (1.0 + gate * (1.0 - sig))).astype(BF)
    dup = (dhidden * gate * sig).astype(BF)
    dn2 = lax.psum_scatter(
        (dot_t(dgate, w_gate) + dot_t(dup, w_up)).astype(BF),
        "tensor",
        scatter_dimension=0,
        tiled=True,
    ).astype(F32)
    grad_gate = t_dot(normed_two_all, dgate)
    grad_up = t_dot(normed_two_all, dup)
    grad_gate, grad_up, grad_down = (
        lax.psum(g.astype(BF), "dp").astype(F32) for g in (grad_gate, grad_up, grad_down)
    )
    grad_ffn_gain = jnp.sum(dn2 * middle * factor_two, 0)
    dmiddle = cot + norm_back(dn2, middle, factor_two, ffn_gain)

    da = dmiddle.astype(BF)
    grad_out_t = t_dot(da, attended).astype(BF)
    dattended = dot_t(da, out_full).astype(BF)
    dq_rot, dk_part, dv_part = attend_back(
        q_low, k_seq, v_seq, start, prefix_len, lse, dattended
    )
    dkv = lax.psum_scatter(
        jnp.concatenate(
            [dk_part.reshape(SEQ_LEN, kv_all), dv_part.reshape(SEQ_LEN, kv_all)], 1
        ).astype(BF),
        "tensor",
        scatter_dimension=0,
        tiled=True,
        axis_index_groups=seq_groups,
    ).astype(F32)
    dq_normed = unrotate(dq_rot, cosine, sine)
    dk_normed = unrotate(
        dkv[:, :kv_all].reshape(rows, KEY_VALUE_HEADS, HEAD_SIZE), cosine, sine
    )
    grad_query_gain = jnp.sum(dq_normed * q_raw * q_factor, (0, 1))
    grad_key_gain = jnp.sum(dk_normed * k_raw * k_factor, (0, 1))
    dq = norm_back(dq_normed, q_raw, q_factor, query_gain).reshape(rows, q_all).astype(BF)
    dk = norm_back(dk_normed, k_raw, k_factor, key_gain).reshape(rows, kv_all).astype(BF)
    dv = dkv[:, kv_all:].astype(BF)
    dn1 = dot_t(dq, query_full) + dot_t(dk, key_weight) + dot_t(dv, value_weight)
    grad_attn_gain = jnp.sum(dn1 * source * factor_one, 0)
    grad_tokens = dmiddle + norm_back(dn1, source, factor_one, attn_gain)
    grad_query = t_dot(normed, dq).astype(BF)
    grad_kv = t_dot(normed, jnp.concatenate([dk, dv], 1)).astype(BF)

    wide = jnp.concatenate([grad_query, grad_out_t, grad_kv], 1)
    wide = lax.psum_scatter(wide, "dp", scatter_dimension=0, tiled=True)
    parts = jnp.concatenate(
        [
            wide[:, : 2 * q_all].reshape(cut, 2, t_size, q_dev).transpose(0, 2, 1, 3).reshape(cut, t_size, 2 * q_dev),
            wide[:, 2 * q_all :].reshape(cut, t_size, 2 * kv_all // t_size),
        ],
        2,
    ).reshape(cut, -1)
    parts = lax.psum_scatter(parts, "tensor", scatter_dimension=1, tiled=True)
    own = lax.all_gather(parts[:, : 2 * q_dev], "dp", axis=0, tiled=True).astype(F32)
    grad_query = own[:, :q_dev]
    grad_out = own[:, q_dev:].T
    kv = (
        lax.all_gather(parts[:, 2 * q_dev :], ("dp", "tensor"), axis=0, tiled=False)
        .reshape(dp_size, t_size, cut, 2 * kv_all // t_size)
        .transpose(0, 2, 1, 3)
        .reshape(width, 2 * kv_all)
        .astype(F32)
    )
    small = sum_small(
        jnp.concatenate(
            [
                grad_attn_gain,
                grad_ffn_gain,
                grad_query_gain,
                grad_key_gain,
                jnp.broadcast_to(squares, (128,)),
            ]
        )
    )
    loss = small[2 * width + 2 * HEAD_SIZE] / (count * width)
    return (
        result.astype(BF),
        loss,
        grad_tokens,
        grad_query,
        kv[:, :kv_all],
        kv[:, kv_all:],
        small[2 * width : 2 * width + HEAD_SIZE],
        small[2 * width + HEAD_SIZE : 2 * width + 2 * HEAD_SIZE],
        grad_out,
        small[:width],
        small[width : 2 * width],
        grad_gate,
        grad_up,
        grad_down,
    )


def solution(mesh):
    rows, cols, whole = P(("dp", "tensor"), None), P(None, "tensor"), P()
    down = P("tensor", None)
    return jax.shard_map(
        body,
        mesh=mesh,
        in_specs=(
            rows, rows, P(("dp", "tensor")), P("dp"), cols, whole, whole, whole, whole,
            down, whole, whole, cols, cols, down,
        ),
        out_specs=(
            rows, whole, rows, cols, whole, whole, whole, whole, down, whole, whole,
            cols, cols, down,
        ),
        check_vma=False,
    )
```
